128 devices in a mesh: comp: 8 (over z_lo, x), lon: 16 (over y, z_hi, core).
Axes of the slice: x: 4, y: 4, z: 4 (z_hi: 2, z_lo: 2; z = z_hi * 2 + z_lo), core: 2. Of those that a mesh axis runs over, the one named last changes fastest.
Arguments:
- fluxes: bfloat16 [10, 128, 12288], P(None, ('comp', 'lon')), may hold values from -6 to 6
- tracers: float32 [3, 40, 128, 10240], P(None, None, 'comp', 'lon'), may hold values from -6 to 6
- diffusivity: float32 [40, 128, 10240], P(None, 'comp', 'lon'), may hold values from 0.01 to 0.05
- east_speed: float32 [40, 128, 10240], P(None, 'comp', 'lon'), may hold values from -0.2 to 0.2
- north_speed: float32 [40, 128, 10240], P(None, 'comp', 'lon'), may hold values from -0.2 to 0.2
- wet: int32 [128, 10240], P('comp', 'lon'), may hold values 0 or 1
- coupling: float32 [3, 10], replicated, may hold values from -2 to 2
- sources: int32 [10240, 4], P(('comp', 'lon')), may hold values from 0 to 95, as said below
- live_slots: int32 [10240], P(('comp', 'lon')), may hold values from 1 to 4, as said below
- tiles: bfloat16 [10240, 4, 128, 128], P(('comp', 'lon')), may hold values from -0.25 to 0.25
Outputs:
- ocean: float32 [3, 40, 128, 10240], P(None, None, 'comp', 'lon')
The draws below stay inside these ranges and needn't reach their ends.
Inputs may be any that keep to these rules, and one draw needn't show every extreme that they name: `sources`: a source block of the atmosphere rows of the target's comp band within the target's lon block. Slots k < live_slots[t] count, the others are padding.
All inputs are finite; a program needn't handle non-finite values. No bound on the sum of `wet` on one device may be relied on, other than what follows from the above.
Results may differ from the reference program's by a relative error of at most 0.009.
Values may be sent and summed in bfloat16 or wider, within the bound.
No kernel may reach another device: no remote copies, remote signals or barrier semaphores. Data moves between devices by JAX's collectives and lax.ppermute only.
A program may use at most 192 MiB of HBM per device.

```python
import math
import jax
import jax.numpy as jnp
from jax import lax

FIELDS = 10
TRACERS = 3
LEV = 40
BLK = 128
SLOTS = 4
ALON_BLK = 768
OLAT_DEV = 16
OLON_DEV = 640
ALON = 12288
AROWS = 128
NY = 128
NX = 10240
SRC_ROWS = 16
SRC_BLOCKS = 96
TB_DEV = 80
TARGETS = 10240
N_COMP = 8
N_LON = 16


def draw_sources(key, part):
    segs = OLON_DEV // BLK
    per_row = ALON_BLK // BLK
    local = jnp.arange(TARGETS, dtype=jnp.int32) % TB_DEV
    row_base = local // segs * SRC_ROWS // OLAT_DEV
    col_base = local % segs * per_row // segs
    key_row, key_col = jax.random.split(jax.random.fold_in(key, 11))
    row_jump = jax.random.randint(key_row, (TARGETS, SLOTS), 0, 2, dtype=jnp.int32)
    col_jump = jax.random.randint(key_col, (TARGETS, SLOTS), 0, 2, dtype=jnp.int32)
    rows = jnp.minimum(row_base[:, None] + row_jump, SRC_ROWS - 1)
    cols = jnp.minimum(col_base[:, None] + col_jump, per_row - 1)
    index = rows * per_row + cols
    slot = jnp.arange(SLOTS, dtype=jnp.int32)[None, :]
    first = (local[:, None] == 0) & (slot == 0)
    last = (local[:, None] == TB_DEV - 1) & (slot == 0)
    index = jnp.where(first, 0, jnp.where(last, SRC_BLOCKS - 1, index))
    return index.astype(jnp.int32)


def draw_live_slots(key, part):
    local = jnp.arange(TARGETS, dtype=jnp.int32) % TB_DEV
    counts = jax.random.randint(jax.random.fold_in(key, 23), (TARGETS,), 1, SLOTS + 1, dtype=jnp.int32)
    counts = jnp.where(local == 0, SLOTS, jnp.where(local == 1, 1, counts))
    return counts.astype(jnp.int32)


def plant(entries, own_key, least, high):
    shape = entries.shape
    place = [jax.random.randint(jax.random.fold_in(own_key, axis), (), 0, shape[axis]) for axis in range(len(shape))]
    entries = entries.at[tuple(place)].set(least)
    longest = shape.index(max(shape))
    place[longest] = (place[longest] + 1) % shape[longest]
    return entries.at[tuple(place)].set(high)


def steps_of(own_key, extent, cuts, smallest, high):
    factor_of, own = 1.0, jax.random.fold_in(own_key, 6)
    for dim, blocks in cuts:
        steps = jnp.exp(jax.random.uniform(jax.random.fold_in(own, dim), (blocks,), jnp.float32, smallest / len(cuts), high / len(cuts)))
        factor_of = factor_of * jnp.repeat(steps, extent[dim] // blocks).reshape([-1 if axis == dim else 1 for axis in range(len(extent))])
    return factor_of


def gaussian(stream_key, shape, deviation, bound, cuts=(), held_as=jnp.bfloat16):
    loudness = steps_of(stream_key, shape, cuts, -0.22, 0.18) if cuts else 1.0
    values = jax.random.normal(stream_key, shape, jnp.float32) * deviation * loudness
    return jnp.minimum(jnp.maximum(values, -bound), bound).astype(held_as)


def setup_inputs(seed: int = 0) -> dict:
    arg_keys = jax.random.split(jax.random.key(seed), 11)
    return {
        "fluxes": gaussian(arg_keys[0], (FIELDS, AROWS, ALON), 1.0, 6.0, ((1, 128),)),
        "tracers": gaussian(arg_keys[1], (TRACERS, LEV, NY, NX), 1.0, 6.0, ((2, 8), (3, 16)), jnp.float32),
        "diffusivity": jnp.clip(jnp.exp(math.log(0.05) - 1.609438 * jax.random.uniform(arg_keys[2], (LEV, NY, NX), jnp.float32) ** steps_of(arg_keys[2], (LEV, NY, NX), ((1, 8), (2, 16)), -0.2, 0.2)), 0.01, 0.05),
        "east_speed": jnp.clip(jax.random.uniform(arg_keys[3], (LEV, NY, NX), jnp.float32, -0.2, 0.2) * steps_of(arg_keys[3], (LEV, NY, NX), ((1, 8), (2, 16)), -0.4, 0.0), -0.2, 0.2),
        "north_speed": jnp.clip(jax.random.uniform(arg_keys[4], (LEV, NY, NX), jnp.float32, -0.2, 0.2) * steps_of(arg_keys[4], (LEV, NY, NX), ((1, 8), (2, 16)), -0.4, 0.0), -0.2, 0.2),
        "wet": plant((jax.random.randint(arg_keys[5], (NY, NX), 0, 10) < 7).astype(jnp.int32), jax.random.fold_in(arg_keys[5], 1), 0, 1),
        "coupling": gaussian(arg_keys[6], (TRACERS, FIELDS), FIELDS ** -0.5, 2.0, (), jnp.float32),
        "sources": draw_sources(jax.random.fold_in(arg_keys[10], 71), 0),
        "live_slots": draw_live_slots(jax.random.fold_in(arg_keys[10], 71), 0),
        "tiles": gaussian(arg_keys[9], (TARGETS, SLOTS, BLK, BLK), (BLK * SLOTS) ** -0.5, 0.25, ((0, 128),)),
    }


VMIX = 0.2


def transport(field, kap, east, north, wetf):
    pair_x = wetf[:, :-1] * wetf[:, 1:]
    diff_x = 0.5 * (kap[..., :-1] + kap[..., 1:]) * pair_x
    speed_x = east[..., :-1] * pair_x
    flux_x = jnp.maximum(speed_x, 0.0) * field[..., :-1] + jnp.minimum(speed_x, 0.0) * field[..., 1:] - diff_x * (field[..., 1:] - field[..., :-1])
    pair_y = wetf[:-1, :] * wetf[1:, :]
    diff_y = 0.5 * (kap[..., :-1, :] + kap[..., 1:, :]) * pair_y
    speed_y = north[..., :-1, :] * pair_y
    flux_y = jnp.maximum(speed_y, 0.0) * field[..., :-1, :] + jnp.minimum(speed_y, 0.0) * field[..., 1:, :] - diff_y * (field[..., 1:, :] - field[..., :-1, :])
    inner = field[..., 1:-1, 1:-1]
    spread = flux_x[..., 1:-1, 1:] - flux_x[..., 1:-1, :-1] + flux_y[..., 1:, 1:-1] - flux_y[..., :-1, 1:-1]
    column = wetf[1:-1, 1:-1]
    down = VMIX * (inner[:, 1:] - inner[:, :-1]) * column
    zeros = jnp.zeros_like(inner[:, :1])
    mixing = jnp.concatenate([down, zeros], axis=1) - jnp.concatenate([zeros, down], axis=1)
    return inner - spread + mixing


def padded(array, mode_y):
    lead = [(0, 0)] * (array.ndim - 2)
    out = jnp.pad(array, lead + [(1, 1), (0, 0)], mode=mode_y)
    return jnp.pad(out, lead + [(0, 0), (1, 1)], mode="wrap")


def reference(fluxes, tracers, diffusivity, east_speed, north_speed, wet, coupling, sources, live_slots, tiles):
    per_row = ALON_BLK // BLK
    segs = OLON_DEV // BLK
    devices = N_COMP * N_LON
    blocks = fluxes.reshape(FIELDS, N_COMP, SRC_ROWS, N_LON, per_row, BLK)
    blocks = blocks.transpose(1, 3, 2, 4, 0, 5).reshape(devices, SRC_BLOCKS, FIELDS, BLK)
    picks = sources.reshape(devices, TB_DEV * SLOTS)
    counts = live_slots.reshape(devices, TB_DEV)
    weights = tiles.reshape(devices, TB_DEV, SLOTS, BLK, BLK)

    def remap_one(items):
        block_set, pick, count, weight = items
        gathered = jnp.take(block_set, pick, axis=0).reshape(TB_DEV, SLOTS, FIELDS, BLK).astype(jnp.float32)
        alive = (jnp.arange(SLOTS, dtype=jnp.int32)[None, :] < count[:, None]).astype(jnp.float32)
        gathered = gathered * alive[:, :, None, None]
        return jnp.einsum("tkfa,tkab->tfb", gathered, weight.astype(jnp.float32), precision=lax.Precision.HIGHEST)

    remapped = lax.map(remap_one, (blocks, picks, counts, weights))
    surface = remapped.reshape(N_COMP, N_LON, OLAT_DEV, segs, FIELDS, BLK)
    surface = surface.transpose(4, 0, 2, 1, 3, 5).reshape(FIELDS, NY, NX)
    wetf = wet.astype(jnp.float32)
    forcing = jnp.einsum("rf,fyx->ryx", coupling, surface, precision=lax.Precision.HIGHEST) * wetf
    kap = padded(diffusivity, "edge")
    east = padded(east_speed, "constant")
    north = padded(north_speed, "constant")
    wet_pad = padded(wetf, "constant")
    first = transport(padded(tracers, "constant"), kap, east, north, wet_pad)
    first = first.at[:, 0].add(forcing)
    ocean = transport(padded(first, "constant"), kap, east, north, wet_pad)
    return ocean.at[:, 0].add(forcing)
```

```python
import functools

import jax
import jax.numpy as jnp
from jax import lax
from jax.experimental import pallas as pl
from jax.experimental.pallas import tpu as pltpu
from jax.sharding import PartitionSpec as P

VMIX = 0.2
L = 128
F32 = jnp.float32
BF = jnp.bfloat16
ANY = pl.BlockSpec(memory_space=pltpu.HBM)
VM = pl.BlockSpec(memory_space=pltpu.VMEM)
SM = pl.BlockSpec(memory_space=pltpu.SMEM)
NB, NR, NZ, NY = 5, 3, 40, 16
NQ = NR * NZ
ZP = NZ + 2


def lanes(rows=NY):
    return lax.broadcasted_iota(jnp.int32, (rows, L), 1)


def subl(rows=NY):
    return lax.broadcasted_iota(jnp.int32, (rows, L), 0)


def col(b):
    return slice(b * L, (b + 1) * L)


def east_of(vals, rows=8):
    rolled = [pltpu.roll(v, L - 1, 1) for v in vals]
    last = lanes(rows) == L - 1
    return [jnp.where(last, rolled[b + 1], rolled[b]) if b < NB - 1 else rolled[b] for b in range(NB)]


def west_of(vals, rows=8):
    rolled = [pltpu.roll(v, 1, 1) for v in vals]
    head = lanes(rows) == 0
    return [jnp.where(head, rolled[b - 1], rolled[b]) if b else rolled[b] for b in range(NB)]


def every2(flat, at):
    return flat[pl.ds(at, 8, stride=2), :]


def bcast(ref, b, j):
    return jnp.broadcast_to(ref[b, pl.ds(j, 1), :], (8, L))


def pack_ns_kernel(idx, q_h, k_h, n_h, wet_h, ns1, ns2, q_v, k_v, n_v, wet_i, rows_n, rows_s, sem):
    cw = pltpu.make_async_copy(wet_h, wet_i, sem.at[0])
    cw.start()
    copies = []
    for b in range(NB):
        at = pl.ds(b * L, L)
        copies.append(pltpu.make_async_copy(q_h.at[:, :, :, at], q_v.at[b], sem.at[1 + 3 * b]))
        copies.append(pltpu.make_async_copy(k_h.at[:, :, at], k_v.at[b], sem.at[2 + 3 * b]))
        copies.append(pltpu.make_async_copy(n_h.at[:, :, at], n_v.at[b], sem.at[3 + 3 * b]))
    for cp in copies:
        cp.start()
    cw.wait()
    even = idx[0] == 1
    for b in range(NB):
        for cp in copies[3 * b : 3 * b + 3]:
            cp.wait()
        for ref, count, base in ((q_v, NQ, 0), (k_v, NZ, NQ), (n_v, NZ, NQ + NZ)):
            flat = ref.reshape(NB * count * NY, L)
            for g in range(0, count, 8):
                at = (b * count + g) * NY
                rows_n[base + g : base + g + 8, :] = flat[pl.ds(at + NY - 1, 8, stride=NY), :]
                rows_s[base + g : base + g + 8, :] = flat[pl.ds(at, 8, stride=NY), :]
        w = wet_i[:, col(b)].astype(F32)
        rows_n[200:208, :] = jnp.broadcast_to(w[NY - 1 : NY, :], (8, L))
        rows_s[200:208, :] = jnp.broadcast_to(w[0:1, :], (8, L))
        for g in range(0, 208, 16):
            n, s = rows_n[g : g + 16, :], rows_s[g : g + 16, :]
            ns1[b, g : g + 16, :] = jnp.where(even, n, s).astype(BF)
            ns2[b, g : g + 16, :] = jnp.where(even, s, n).astype(BF)


def pack_lon_kernel(idx, flux_h, q_h, k_h, e_h, wet_h, after, a2a, hown, flux, q_v, k_v, e_v, wet_i, sem):
    pairs = [
        (flux_h, flux), (wet_h, wet_i),
        (q_h.at[:, :, :, pl.ds(4 * L, L)], q_v.at[1]), (q_h.at[:, :, :, pl.ds(0, L)], q_v.at[0]),
        (k_h.at[:, :, pl.ds(4 * L, L)], k_v.at[1]), (k_h.at[:, :, pl.ds(0, L)], k_v.at[0]),
        (e_h.at[:, :, pl.ds(4 * L, L)], e_v),
    ]
    copies = [pltpu.make_async_copy(a, b, sem.at[n]) for n, (a, b) in enumerate(pairs)]
    for cp in copies:
        cp.start()
    copies[0].wait()
    pad = jnp.zeros((6, L), BF)
    for d in range(16):
        for m in range(6):
            a2a[d, m] = jnp.concatenate([flux[:, col(d * 6 + m)], pad], axis=0)
    for cp in copies[1:]:
        cp.wait()
    lane = lanes()
    zero = jnp.zeros((NY, L), F32)

    def edge(z, carry):
        e0, e1, w0, w1 = carry
        for r in range(NR):
            j = r * NZ + z
            here = lane == j
            e0 = jnp.where(here, pltpu.roll(q_v[1, r, z], j + 1, 1), e0)
            w0 = jnp.where(here, pltpu.roll(q_v[0, r, z], j, 1), w0)
        here = lane == z
        e1 = jnp.where(here, pltpu.roll(k_v[1, z], z + 1, 1), e1)
        w1 = jnp.where(here, pltpu.roll(k_v[0, z], z, 1), w1)
        e1 = jnp.where(lane == z + NZ, pltpu.roll(e_v[z], z + NZ + 1, 1), e1)
        return e0, e1, w0, w1

    e0, e1, w0, w1 = lax.fori_loop(0, NZ, edge, (zero, zero, zero, zero), unroll=4)
    e0 = jnp.where(lane == NQ, pltpu.roll(wet_i[:, col(4)].astype(F32), NQ + 1, 1), e0)
    w0 = jnp.where(lane == NQ, pltpu.roll(wet_i[:, col(0)].astype(F32), NQ, 1), w0)
    hown[0], hown[1], hown[2], hown[3] = e0, e1, w0, w1
    l_east, l_west = idx[2], idx[3]
    a2a[l_east, 6] = e0.astype(BF)
    a2a[l_east, 7] = e1.astype(BF)
    a2a[l_west, 6] = w0.astype(BF)
    a2a[l_west, 7] = w1.astype(BF)


def stencil(flat, coef, z, halo_n, halo_s, vv, put):
    zu, zd = jnp.maximum(z - 1, 0), jnp.minimum(z + 1, NZ - 1)
    c0, ce, cw, cn, cs = coef
    sub = subl(8)
    for r in range(NR):
        def at(b, zz):
            return pl.multiple_of(((b * NR + r) * ZP + zz + 1) * NY, NY)

        ev = [every2(flat, at(b, z)) for b in range(NB)]
        od = [every2(flat, at(b, z) + 1) for b in range(NB)]
        east = [east_of(ev), east_of(od)]
        west = [west_of(ev), west_of(od)]
        j = r * NZ + z
        for b in range(NB):
            north_od = jnp.where(sub == 7, bcast(halo_n, b, j), every2(flat, at(b, z) + 2))
            south_ev = jnp.where(sub == 0, bcast(halo_s, b, j), every2(flat, at(b, z) - 1))
            north, south = (od[b], north_od), (south_ev, ev[b])
            outs = []
            for h, q in enumerate((ev[b], od[b])):
                out = c0[b][h] * q + ce[b][h] * east[h][b] + cw[b][h] * west[h][b]
                out = out + cn[b][h] * north[h] + cs[b][h] * south[h]
                outs.append(out + vv[b][h] * (every2(flat, at(b, zu) + h) + every2(flat, at(b, zd) + h)))
            put(b, r, j, outs)


CH = 8


def step1_kernel(
    idx, r1, r2, wet_h, q_h, k_h, e_h, n_h,
    first, coefs, rows, cols,
    q_v, k_v, e_v, n_v, f_v, c_v, wet_i, w_v, hn, hs, pe, pn, an0, bn0, sem, osem,
):
    cw = pltpu.make_async_copy(wet_h, wet_i, sem.at[NZ // CH, 0])
    cw.start()

    def fetch(i):
        out, z0 = [], i * CH
        zs = pl.ds(z0, CH)
        for b in range(NB):
            at = pl.ds(b * L, L)
            out.append(pltpu.make_async_copy(q_h.at[:, zs, :, at], q_v.at[b, :, pl.ds(z0 + 1, CH)], sem.at[i, 4 * b]))
            out.append(pltpu.make_async_copy(k_h.at[zs, :, at], k_v.at[b, pl.ds(z0 + 1, CH)], sem.at[i, 4 * b + 1]))
            out.append(pltpu.make_async_copy(e_h.at[zs, :, at], e_v.at[b, zs], sem.at[i, 4 * b + 2]))
            out.append(pltpu.make_async_copy(n_h.at[zs, :, at], n_v.at[b, zs], sem.at[i, 4 * b + 3]))
        return out

    def store(i):
        z0 = i * CH
        return [
            pltpu.make_async_copy(f_v.at[:, :, pl.ds(z0, CH)], first.at[:, :, pl.ds(z0 + 1, CH)], osem.at[i, 0]),
            pltpu.make_async_copy(c_v.at[:, :, pl.ds(z0, CH)], coefs.at[:, :, pl.ds(z0, CH)], osem.at[i, 1]),
        ]

    for i in range(NZ // CH):
        for cp in fetch(i):
            cp.start()
    even = idx[0] == 1
    for g in range(0, 208, 16):
        a, c = r1[:, g : g + 16, :].astype(F32), r2[:, g : g + 16, :].astype(F32)
        hn[:, g : g + 16, :] = jnp.where(even, a, c)
        hs[:, g : g + 16, :] = jnp.where(even, c, a)
    cw.wait()
    for b in range(NB):
        w_v[b] = wet_i[:, col(b)].astype(F32)
    wflat = w_v.reshape(NB * NY, L)
    w = [[every2(wflat, b * NY + h) for b in range(NB)] for h in range(2)]
    sub, lane = subl(8), lanes(8)
    we = [east_of(w[0]), east_of(w[1])]
    for b in range(NB):
        hw = jnp.broadcast_to(hn[b, 200:201, :], (8, L))
        wn = (w[1][b], jnp.where(sub == 7, hw, pltpu.roll(w[0][b], 7, 0)))
        for h in range(2):
            p = w[h][b] * we[h][b]
            pe[b, h] = jnp.where(lane == L - 1, 0.0, p) if b == NB - 1 else p
            pn[b, h] = w[h][b] * wn[h]
    for cp in fetch(0):
        cp.wait()

    def level(z, carry):
        he, hw = carry
        kflat = k_v.reshape(NB * ZP * NY, L)
        eflat, nflat = e_v.reshape(NB * NZ * NY, L), n_v.reshape(NB * NZ * NY, L)
        ks, ns = [[], []], [[], []]
        ae, be = [[], []], [[], []]
        for b in range(NB):
            at = pl.multiple_of((b * ZP + z + 1) * NY, NY)
            for h in range(2):
                ks[h].append(every2(kflat, at + h))
        for h in range(2):
            ke = east_of(ks[h])
            for b in range(NB):
                at = pl.multiple_of((b * NZ + z) * NY, NY)
                d = 0.5 * (ks[h][b] + ke[b]) * pe[b, h]
                u = every2(eflat, at + h) * pe[b, h]
                ae[h].append(jnp.maximum(u, 0.0) + d)
                be[h].append(jnp.minimum(u, 0.0) - d)
        aw, bw = [west_of(ae[0]), west_of(ae[1])], [west_of(be[0]), west_of(be[1])]
        coef = [[], [], [], [], []]
        vv = []
        for b in range(NB):
            at = pl.multiple_of((b * ZP + z + 1) * NY, NY)
            kn = (ks[1][b], jnp.where(sub == 7, bcast(hn, b, NQ + z), every2(kflat, at + 2)))
            at = pl.multiple_of((b * NZ + z) * NY, NY)
            an, bn = [], []
            for h in range(2):
                d = 0.5 * (ks[h][b] + kn[h]) * pn[b, h]
                u = every2(nflat, at + h) * pn[b, h]
                an.append(jnp.maximum(u, 0.0) + d)
                bn.append(jnp.minimum(u, 0.0) - d)
            ps = bcast(hs, b, 200) * jnp.broadcast_to(w_v[b, 0:1, :], (8, L))
            d = 0.5 * (bcast(hs, b, NQ + z) + jnp.broadcast_to(ks[0][b][0:1, :], (8, L))) * ps
            u = bcast(hs, b, NQ + NZ + z) * ps
            a_s = (jnp.where(sub == 0, jnp.maximum(u, 0.0) + d, pltpu.roll(an[1], 1, 0)), an[0])
            b_s = (jnp.where(sub == 0, jnp.minimum(u, 0.0) - d, pltpu.roll(bn[1], 1, 0)), bn[0])
            v = [VMIX * every2(wflat, b * NY + h) for h in range(2)]
            vals = []
            for h in range(2):
                a_w, b_w = aw[h][b], bw[h][b]
                if b == 0:
                    a_w, b_w = jnp.where(lane == 0, 0.0, a_w), jnp.where(lane == 0, 0.0, b_w)
                c0 = 1.0 - ae[h][b] + b_w - an[h] + b_s[h] - 2.0 * v[h]
                vals.append((c0, -be[h][b], a_w, -bn[h], a_s[h]))
                for n in range(5):
                    c_v[n, b, z, h] = vals[h][n]
            for n in range(5):
                coef[n].append((vals[0][n], vals[1][n]))
            vv.append(v)
        out = [he, hw]

        def put(b, r, j, outs):
            ff = f_v.reshape(NB * NQ * NY, L)
            at = pl.multiple_of((b * NQ + j) * NY, NY)
            for h in range(2):
                ff[pl.ds(at + h, 8, stride=2), :] = outs[h]
            if b == 0:
                out[1] = tuple(jnp.where(lane == j, pltpu.roll(outs[h], j, 1), out[1][h]) for h in range(2))
            if b == NB - 1:
                out[0] = tuple(jnp.where(lane == j, pltpu.roll(outs[h], j + 1, 1), out[0][h]) for h in range(2))

        stencil(q_v.reshape(NB * NR * ZP * NY, L), coef, z, hn, hs, vv, put)
        return tuple(out)

    zero = jnp.zeros((8, L), F32)
    carry = ((zero, zero), (zero, zero))

    def chunk(i, carry):
        carry = lax.fori_loop(i * CH, (i + 1) * CH - 1, level, carry)

        @pl.when(i < NZ // CH - 1)
        def _():
            for cp in fetch(jnp.minimum(i + 1, NZ // CH - 1)):
                cp.wait()

        carry = level((i + 1) * CH - 1, carry)
        for cp in store(i):
            cp.start()
        return carry

    he, hw = lax.fori_loop(0, NZ // CH, chunk, carry)
    cflat = cols.reshape(2 * NY, L)
    for h in range(2):
        cflat[pl.ds(h, 8, stride=2), :] = he[h]
        cflat[pl.ds(NY + h, 8, stride=2), :] = hw[h]
    ff = f_v.reshape(NB * NQ * NY, L)
    for b in range(NB):
        for g in range(0, NQ, 8):
            at = (b * NQ + g) * NY
            rows[0, b, g : g + 8, :] = ff[pl.ds(at + NY - 1, 8, stride=NY), :]
            rows[1, b, g : g + 8, :] = ff[pl.ds(at, 8, stride=NY), :]
    for i in range(NZ // CH):
        for cp in store(i):
            cp.wait()


def spread3(x):
    x = jnp.where(lanes() < NZ, x, 0.0)
    return x + pltpu.roll(x, NZ, 1) + pltpu.roll(x, 2 * NZ, 1)


def face(w_a, w_b, k_a, k_b, u):
    p = w_a * w_b
    d = 0.5 * (k_a + k_b) * p
    s = u * p
    return spread3(jnp.maximum(s, 0.0) + d), spread3(jnp.minimum(s, 0.0) - d)


def remap_kernel(
    idx, src, live, coup, got, tiles, wet, hown, rows, cols,
    forcing, ns1, ns2, ew1, ew2, hnew, facec, fluxes1,
):
    row = subl()
    zero = jnp.zeros((NY, L), F32)
    cvec = []
    for r in range(NR):
        c = zero
        for f in range(10):
            c = jnp.where(row == f, coup[r, f], c)
        cvec.append(c)

    def target_row(i, _):
        for s in range(NB):
            t = i * NB + s
            n = live[t]
            parts = []
            for k in range(4):
                p = src[k, t]
                blk = got[p // 6 * 8 + p % 6]
                parts.append(jnp.where(k < n, blk, jnp.zeros_like(blk)))
            acc = jnp.dot(jnp.concatenate(parts, axis=1), tiles[t], preferred_element_type=F32)
            for r in range(NR):
                forcing[s, r, pl.ds(i, 1), :] = jnp.sum(acc * cvec[r], axis=0, keepdims=True)
        return 0

    lax.fori_loop(0, NY, target_row, 0, unroll=2)
    for s in range(NB):
        w = wet[:, col(s)].astype(F32)
        for r in range(NR):
            forcing[s, r] = forcing[s, r] * w
    l_east, l_west = idx[2], idx[3]
    oe0, oe1, ow0, ow1 = hown[0], hown[1], hown[2], hown[3]
    ge0, ge1 = got[l_east * 8 + 6].astype(F32), got[l_east * 8 + 7].astype(F32)
    gw0, gw1 = got[l_west * 8 + 6].astype(F32), got[l_west * 8 + 7].astype(F32)

    def wcol(x):
        return jnp.broadcast_to(x[:, NQ : NQ + 1], (NY, L))

    ae, be = face(wcol(oe0), wcol(ge0), oe1, ge1, pltpu.roll(oe1, L - NZ, 1))
    aw, bw = face(wcol(gw0), wcol(ow0), gw1, ow1, pltpu.roll(gw1, L - NZ, 1))
    facec[0], facec[1], facec[2], facec[3] = ae, be, aw, bw
    fe = ae * oe0 + be * ge0
    fw = aw * gw0 + bw * ow0
    fluxes1[0], fluxes1[1] = fe, fw
    lane = lanes()
    he, hw = cols[0] - fe, cols[1] + fw
    for r in range(NR):
        here = lane == r * NZ
        he = he + jnp.where(here, pltpu.roll(forcing[4, r], r * NZ + 1, 1), 0.0)
        hw = hw + jnp.where(here, pltpu.roll(forcing[0, r], r * NZ, 1), 0.0)
    hnew[0], hnew[1] = he, hw
    leven = idx[1] == 1
    ew1[...] = jnp.where(leven, he, hw).astype(BF)
    ew2[...] = jnp.where(leven, hw, he).astype(BF)
    fill = jnp.zeros((L - NY, L), F32)
    fet = jnp.concatenate([fe, fill], axis=0).T
    fwt = jnp.concatenate([fw, fill], axis=0).T
    even = idx[0] == 1
    big = lanes(L)
    sub = subl(L)
    for b in range(NB):
        edges = []
        for side, y in ((0, NY - 1), (1, 0)):
            v = rows[side, b]
            for r in range(NR):
                v = v + jnp.where(sub == r * NZ, jnp.broadcast_to(forcing[b, r, y : y + 1, :], (L, L)), 0.0)
            if b == NB - 1:
                v = v - jnp.where(big == L - 1, jnp.broadcast_to(fet[:, y : y + 1], (L, L)), 0.0)
            if b == 0:
                v = v + jnp.where(big == 0, jnp.broadcast_to(fwt[:, y : y + 1], (L, L)), 0.0)
            edges.append(v)
        n, s = edges
        ns1[b] = jnp.where(even, n, s).astype(BF)
        ns2[b] = jnp.where(even, s, n).astype(BF)


def step2_kernel(
    idx, r1, r2, g1, g2, wet, forcing, hnew, facec, fluxes1, first_in, coefs,
    first, out_h,
    hn, hs, out_v, dl, w_v, sem,
):
    even = idx[0] == 1
    for g in range(0, 128, 16):
        a, c = r1[:, g : g + 16, :].astype(F32), r2[:, g : g + 16, :].astype(F32)
        hn[:, g : g + 16, :] = jnp.where(even, a, c)
        hs[:, g : g + 16, :] = jnp.where(even, c, a)
    leven = idx[1] == 1
    a, c = g1[...].astype(F32), g2[...].astype(F32)
    from_e, from_w = jnp.where(leven, a, c), jnp.where(leven, c, a)
    dl[0] = facec[0] * hnew[0] + facec[1] * from_e
    dl[1] = facec[2] * from_w + facec[3] * hnew[1]
    for b in range(NB):
        w_v[b] = wet[:, col(b)].astype(F32)
    wflat, dflat = w_v.reshape(NB * NY, L), dl.reshape(2 * NY, L)
    lane = lanes()

    def fix(z, _):
        for r in range(NR):
            j = r * NZ + z
            first[4, r, z + 1] = first_in[4, r, z + 1] - jnp.where(
                lane == L - 1, pltpu.roll(fluxes1[0], L - 1 - j, 1), 0.0
            )
            first[0, r, z + 1] = first_in[0, r, z + 1] + jnp.where(lane == 0, pltpu.roll(fluxes1[1], L - j, 1), 0.0)
        return 0

    lax.fori_loop(0, NZ, fix, 0, unroll=4)
    for b in range(NB):
        for r in range(NR):
            first[b, r, 1] = first[b, r, 1] + forcing[b, r]
    lane8 = lanes(8)

    def copy(i, b):
        z0 = i * CH
        return pltpu.make_async_copy(
            out_v.at[b, :, pl.ds(z0, CH)], out_h.at[:, pl.ds(z0, CH), :, pl.ds(b * L, L)], sem.at[i, b]
        )

    def level(z, _):
        coef = [[(coefs[n, b, z, 0], coefs[n, b, z, 1]) for b in range(NB)] for n in range(5)]
        vv = [[VMIX * every2(wflat, b * NY + h) for h in range(2)] for b in range(NB)]

        def put(b, r, j, outs):
            of = out_v.reshape(NB * NQ * NY, L)
            at = pl.multiple_of((b * NQ + j) * NY, NY)
            for h in range(2):
                o = outs[h]
                if b == 0:
                    o = o + jnp.where(lane8 == 0, pltpu.roll(every2(dflat, NY + h), L - j, 1), 0.0)
                if b == NB - 1:
                    o = o - jnp.where(lane8 == L - 1, pltpu.roll(every2(dflat, h), L - 1 - j, 1), 0.0)
                of[pl.ds(at + h, 8, stride=2), :] = o

        stencil(first.reshape(NB * NR * ZP * NY, L), coef, z, hn, hs, vv, put)
        return 0

    def chunk(i, _):
        lax.fori_loop(i * CH, (i + 1) * CH, level, 0)

        @pl.when(i == 0)
        def _():
            for b in range(NB):
                for r in range(NR):
                    out_v[b, r, 0] = out_v[b, r, 0] + forcing[b, r]

        for b in range(NB):
            copy(i, b).start()
        return 0

    lax.fori_loop(0, NZ // CH, chunk, 0)
    for i in range(NZ // CH):
        for b in range(NB):
            copy(i, b).wait()


def hbm(x):
    return pltpu.with_memory_space_constraint(x, pltpu.HBM)


def vmem(x):
    return pltpu.with_memory_space_constraint(x, pltpu.VMEM)


def shards(
    fluxes, tracers, diffusivity, east_speed, north_speed, wet, coupling, sources, live_slots, tiles
):
    sds = jax.ShapeDtypeStruct
    band, lon = lax.axis_index("comp"), lax.axis_index("lon")
    n_lon = lax.axis_size("lon")
    idx = jnp.stack([1 - band % 2, 1 - lon % 2, (lon + 1) % n_lon, (lon + n_lon - 1) % n_lon]).astype(jnp.int32)
    dma = pltpu.SemaphoreType.DMA
    q5, s5 = (NB, NR, NZ, NY, L), (NB, NZ, NY, L)
    qp, cf = (NB, NR, ZP, NY, L), (5, NB, NZ, 2, 8, L)
    rowpay, edgepay = (NB, 208, L), (NB, 128, L)

    def params(mib):
        return pltpu.CompilerParams(vmem_limit_bytes=mib << 20)

    flux, q, k, e, n, wh = map(
        hbm, (fluxes[:, 0, :], tracers, diffusivity, east_speed, north_speed, wet)
    )
    ns1, ns2 = pl.pallas_call(
        pack_ns_kernel,
        out_shape=(sds(rowpay, BF), sds(rowpay, BF)),
        in_specs=[SM] + [ANY] * 4,
        out_specs=(VM,) * 2,
        scratch_shapes=[
            pltpu.VMEM(q5, F32), pltpu.VMEM(s5, F32), pltpu.VMEM(s5, F32), pltpu.VMEM((NY, 640), jnp.int32),
            pltpu.VMEM((208, L), F32), pltpu.VMEM((208, L), F32), dma((16,)),
        ],
        compiler_params=params(16),
        name="pack_ns",
    )(idx, q, k, n, wh)
    swap_a = [(i, i ^ 1) for i in range(8)]
    swap_b = [(i, i + 1) for i in (1, 3, 5)] + [(i + 1, i) for i in (1, 3, 5)]
    r1 = lax.ppermute(ns1, "comp", swap_a)
    r2 = lax.ppermute(ns2, "comp", swap_b)
    a2a, hown = pl.pallas_call(
        pack_lon_kernel,
        out_shape=(sds((16, 8, NY, L), BF), sds((4, NY, L), F32)),
        in_specs=[SM] + [ANY] * 5 + [pl.BlockSpec(memory_space=pl.ANY)],
        out_specs=(VM,) * 2,
        scratch_shapes=[
            pltpu.VMEM((10, 12288), BF), pltpu.VMEM((2, NR, NZ, NY, L), F32), pltpu.VMEM((2, NZ, NY, L), F32),
            pltpu.VMEM((NZ, NY, L), F32), pltpu.VMEM((NY, 640), jnp.int32), dma((7,)),
        ],
        compiler_params=params(12),
        name="pack_lon",
    )(idx, flux, q, k, e, wh, ns1)
    got = lax.all_to_all(a2a, "lon", split_axis=0, concat_axis=0, tiled=True)
    first, coefs, rows, cols = pl.pallas_call(
        step1_kernel,
        out_shape=(sds(qp, F32), sds(cf, F32), sds((2,) + edgepay, F32), sds((2, NY, L), F32)),
        in_specs=[SM] + [VM] * 2 + [ANY] * 5,
        out_specs=(pl.BlockSpec(memory_space=pl.ANY),) * 2 + (VM,) * 2,
        scratch_shapes=[
            pltpu.VMEM(qp, F32), pltpu.VMEM((NB, ZP, NY, L), F32), pltpu.VMEM(s5, F32), pltpu.VMEM(s5, F32),
            pltpu.VMEM(q5, F32), pltpu.VMEM(cf, F32), pltpu.VMEM((NY, 640), jnp.int32), pltpu.VMEM((NB, NY, L), F32),
            pltpu.VMEM(rowpay, F32), pltpu.VMEM(rowpay, F32),
            pltpu.VMEM((NB, 2, 8, L), F32), pltpu.VMEM((NB, 2, 8, L), F32),
            pltpu.VMEM((8, L), F32), pltpu.VMEM((8, L), F32),
            dma((NZ // CH + 1, 4 * NB)), dma((NZ // CH, 2)),
        ],
        compiler_params=params(32),
        name="step1",
    )(idx, r1, r2, wh, q, k, e, n)
    forcing, ms1, ms2, ew1, ew2, hnew, facec, fluxes1 = pl.pallas_call(
        remap_kernel,
        out_shape=(
            sds((NB, NR, NY, L), F32), sds(edgepay, BF), sds(edgepay, BF), sds((NY, L), BF), sds((NY, L), BF),
            sds((2, NY, L), F32), sds((4, NY, L), F32), sds((2, NY, L), F32),
        ),
        in_specs=[SM] * 4 + [VM] * 6,
        out_specs=(VM,) * 8,
        compiler_params=params(6),
        name="remap",
    )(idx, sources.T, live_slots, coupling, got.reshape(128, NY, L), vmem(tiles.reshape(80, 512, L)), wet, hown, rows, cols)
    lon_a = [(i, i ^ 1) for i in range(16)]
    lon_b = [((2 * i + 1) % 16, (2 * i + 2) % 16) for i in range(8)]
    lon_b = lon_b + [(b, a) for a, b in lon_b]
    r1 = lax.ppermute(ms1, "comp", swap_a)
    r2 = lax.ppermute(ms2, "comp", swap_b)
    g1 = lax.ppermute(ew1, "lon", lon_a)
    g2 = lax.ppermute(ew2, "lon", lon_b)
    return pl.pallas_call(
        step2_kernel,
        out_shape=(pltpu.VMEM(qp, F32), sds(tracers.shape, F32)),
        in_specs=[SM] + [VM] * 11,
        out_specs=(VM, ANY),
        scratch_shapes=[
            pltpu.VMEM(edgepay, F32), pltpu.VMEM(edgepay, F32), pltpu.VMEM(q5, F32),
            pltpu.VMEM((2, NY, L), F32), pltpu.VMEM((NB, NY, L), F32), dma((NZ // CH, NB)),
        ],
        input_output_aliases={10: 0},
        compiler_params=params(10),
        name="step2",
    )(idx, r1, r2, g1, g2, wet, forcing, hnew, facec, fluxes1, vmem(first), vmem(coefs))[1]


def solution(mesh):
    return jax.shard_map(
        shards,
        mesh=mesh,
        in_specs=(
            P(None, ("comp", "lon"), None),
            P(None, None, "comp", "lon"),
            P(None, "comp", "lon"),
            P(None, "comp", "lon"),
            P(None, "comp", "lon"),
            P("comp", "lon"),
            P(),
            P(("comp", "lon"), None),
            P(("comp", "lon")),
            P(("comp", "lon"), None, None, None),
        ),
        out_specs=P(None, None, "comp", "lon"),
        check_vma=False,
    )
```

```python
import functools

import jax
import jax.numpy as jnp
from jax import lax
from jax.experimental import pallas as pl
from jax.experimental.pallas import tpu as pltpu
from jax.sharding import PartitionSpec as P

VMIX = 0.2
L = 128
F32 = jnp.float32
BF = jnp.bfloat16
ANY = pl.BlockSpec(memory_space=pltpu.HBM)
VM = pl.BlockSpec(memory_space=pltpu.VMEM)
SM = pl.BlockSpec(memory_space=pltpu.SMEM)
NB, NR, NZ, NY = 5, 3, 40, 16
NQ = NR * NZ
CH = 8
NC = NZ // CH
UNROLL1 = 2


def lanes(rows=NY):
    return lax.broadcasted_iota(jnp.int32, (rows, L), 1)


def subl(rows=NY):
    return lax.broadcasted_iota(jnp.int32, (rows, L), 0)


def col(b):
    return slice(b * L, (b + 1) * L)


def east_of(vals):
    rolled = [pltpu.roll(v, L - 1, 1) for v in vals]
    last = lanes() == L - 1
    return [jnp.where(last, rolled[b + 1], rolled[b]) if b < NB - 1 else rolled[b] for b in range(NB)]


def west_of(vals, wrap=False):
    rolled = [pltpu.roll(v, 1, 1) for v in vals]
    head = lanes() == 0
    return [jnp.where(head, rolled[b - 1], rolled[b]) if b or wrap else rolled[b] for b in range(NB)]


def to_lane(acc, val, h, source):
    return jnp.where(lanes() == h, pltpu.roll(val, (h - source) % L, 1), acc)


def pack_kernel(
    idx, flux_h, q_h, k_h, e_h, n_h, wet_h,
    a2a, ns1, ns2, hown, edge_n, edge_s,
    flux, q_v, k_v, n_v, e_v, wet_i, sem,
):
    first_two = [pltpu.make_async_copy(flux_h, flux, sem.at[0]), pltpu.make_async_copy(wet_h, wet_i, sem.at[1])]
    last_e = pltpu.make_async_copy(e_h.at[:, :, pl.ds(4 * L, L)], e_v, sem.at[2])
    copies = {}
    for b in range(NB):
        at = pl.ds(b * L, L)
        copies[b] = [
            pltpu.make_async_copy(q_h.at[:, :, :, at], q_v.at[b], sem.at[3 + 3 * b]),
            pltpu.make_async_copy(k_h.at[:, :, at], k_v.at[b], sem.at[4 + 3 * b]),
            pltpu.make_async_copy(n_h.at[:, :, at], n_v.at[b], sem.at[5 + 3 * b]),
        ]
    for cp in first_two:
        cp.start()
    order = (4, 0, 1, 2, 3)
    for b in order:
        for cp in copies[b]:
            cp.start()
        if b == 4:
            last_e.start()
    for cp in first_two:
        cp.wait()
    pad = jnp.zeros((6, L), BF)
    for d in range(16):
        for m in range(6):
            a2a[d, m] = jnp.concatenate([flux[:, col(d * 6 + m)], pad], axis=0)
    for b in (4, 0):
        for cp in copies[b]:
            cp.wait()
    last_e.wait()
    lane = lanes()
    zero = jnp.zeros((NY, L), F32)

    def edge(i, carry):
        e0, e1, w0, w1 = carry
        acc = [zero] * 9
        for h in range(CH):
            z = i * CH + h
            for r in range(NR):
                acc[r] = to_lane(acc[r], q_v[4, r, z], h, L - 1)
                acc[3 + r] = to_lane(acc[3 + r], q_v[0, r, z], h, 0)
            acc[6] = to_lane(acc[6], k_v[4, z], h, L - 1)
            acc[7] = to_lane(acc[7], e_v[z], h, L - 1)
            acc[8] = to_lane(acc[8], k_v[0, z], h, 0)
        for r in range(NR):
            e0 = e0 + pltpu.roll(acc[r], r * NZ + i * CH, 1)
            w0 = w0 + pltpu.roll(acc[3 + r], r * NZ + i * CH, 1)
        e1 = e1 + pltpu.roll(acc[6], i * CH, 1) + pltpu.roll(acc[7], NZ + i * CH, 1)
        w1 = w1 + pltpu.roll(acc[8], i * CH, 1)
        return e0, e1, w0, w1

    e0, e1, w0, w1 = lax.fori_loop(0, NC, edge, (zero, zero, zero, zero))
    e0 = jnp.where(lane == NQ, pltpu.roll(wet_i[:, col(4)].astype(F32), NQ + 1, 1), e0)
    w0 = jnp.where(lane == NQ, pltpu.roll(wet_i[:, col(0)].astype(F32), NQ, 1), w0)
    hown[0], hown[1], hown[2], hown[3] = e0, e1, w0, w1
    l_east, l_west = idx[2], idx[3]
    a2a[l_east, 6] = e0.astype(BF)
    a2a[l_east, 7] = e1.astype(BF)
    a2a[l_west, 6] = w0.astype(BF)
    a2a[l_west, 7] = w1.astype(BF)
    even = idx[0] == 1
    for b in order:
        if b not in (4, 0):
            for cp in copies[b]:
                cp.wait()
        for ref, count, base in ((q_v, NQ, 0), (k_v, NZ, NQ), (n_v, NZ, NQ + NZ)):
            flat = ref.reshape(NB * count * NY, L)
            for g in range(0, count, 8):
                at = (b * count + g) * NY
                edge_n[b, base + g : base + g + 8, :] = flat[pl.ds(at + NY - 1, 8, stride=NY), :]
                edge_s[b, base + g : base + g + 8, :] = flat[pl.ds(at, 8, stride=NY), :]
        w = wet_i[:, col(b)].astype(F32)
        edge_n[b, 200:208, :] = jnp.broadcast_to(w[NY - 1 : NY, :], (8, L))
        edge_s[b, 200:208, :] = jnp.broadcast_to(w[0:1, :], (8, L))
        for g in range(0, 208, 16):
            n, s = edge_n[b, g : g + 16, :], edge_s[b, g : g + 16, :]
            ns1[b, g : g + 16, :] = jnp.where(even, n, s).astype(BF)
            ns2[b, g : g + 16, :] = jnp.where(even, s, n).astype(BF)


def stencil(get, coef, z, mix, put):
    zu, zd = jnp.maximum(z - 1, 0), jnp.minimum(z + 1, NZ - 1)
    c0, ce, cw, cn, cs = coef
    for r in range(NR):
        q = [get(b, r, z) for b in range(NB)]
        qe, qw = east_of(q), west_of(q)
        j = r * NZ + z
        for b in range(NB):
            qn, qs = pltpu.roll(q[b], NY - 1, 0), pltpu.roll(q[b], 1, 0)
            out = c0[b] * q[b] + ce[b] * qe[b] + cw[b] * qw[b] + cn[b] * qn + cs[b] * qs
            put(b, r, j, out + mix[b] * (get(b, r, zu) + get(b, r, zd)))


def from_sides(idx, r1, r2, at):
    even = idx[0] == 1
    a, c = r1[at].astype(F32), r2[at].astype(F32)
    return jnp.where(even, a, c), jnp.where(even, c, a)


def add_rows(val, south, north):
    sub = subl(8)
    low = val[0:8] + jnp.where(sub == 0, jnp.broadcast_to(south, (8, L)), 0.0)
    high = val[8:16] - jnp.where(sub == 7, jnp.broadcast_to(north, (8, L)), 0.0)
    return jnp.concatenate([low, high], axis=0)


def step1_kernel(
    wet_h, q_h, k_h, e_h, n_h,
    first_h, coefs_h, rows, cols,
    q_v, k_v, e_v, n_v, first, coefs, wet_i, pe, pn, keep, mix, sem, osem,
):
    cw = pltpu.make_async_copy(wet_h, wet_i, sem.at[NC, 0])
    cw.start()

    def fetch(i):
        zs = pl.ds(i * CH, CH)
        return [
            pltpu.make_async_copy(q_h.at[:, zs], q_v.at[:, zs], sem.at[i, 0]),
            pltpu.make_async_copy(k_h.at[zs], k_v.at[zs], sem.at[i, 1]),
            pltpu.make_async_copy(e_h.at[zs], e_v.at[zs], sem.at[i, 2]),
            pltpu.make_async_copy(n_h.at[zs], n_v.at[zs], sem.at[i, 3]),
        ]

    def store(i):
        zs = pl.ds(i * CH, CH)
        return [
            pltpu.make_async_copy(first.at[:, :, zs], first_h.at[:, :, zs], osem.at[i, 0]),
            pltpu.make_async_copy(coefs.at[:, :, zs], coefs_h.at[:, :, zs], osem.at[i, 1]),
        ]

    for i in range(NC):
        for cp in fetch(i):
            cp.start()
    cw.wait()
    row, lane = subl(), lanes()
    w = [wet_i[:, col(b)].astype(F32) for b in range(NB)]
    we = east_of(w)
    for b in range(NB):
        p = w[b] * we[b]
        pe[b] = 0.5 * (jnp.where(lane == L - 1, 0.0, p) if b == NB - 1 else p)
        pn[b] = 0.5 * w[b] * jnp.where(row == NY - 1, 0.0, pltpu.roll(w[b], NY - 1, 0))
        mix[b] = VMIX * w[b]
        keep[b] = 1.0 - 2.0 * VMIX * w[b]
    for cp in fetch(0):
        cp.wait()

    def level(z):
        k = [k_v[z, :, col(b)] for b in range(NB)]
        ke = east_of(k)
        ae, be, an, bn = [], [], [], []
        for b in range(NB):
            kn = pltpu.roll(k[b], NY - 1, 0)
            d = (k[b] + ke[b]) * pe[b]
            u = 2.0 * e_v[z, :, col(b)] * pe[b]
            ae.append(jnp.maximum(u, 0.0) + d)
            be.append(jnp.minimum(u, 0.0) - d)
            d = (k[b] + kn) * pn[b]
            u = 2.0 * n_v[z, :, col(b)] * pn[b]
            an.append(jnp.maximum(u, 0.0) + d)
            bn.append(jnp.minimum(u, 0.0) - d)
        aw, bw = west_of(ae, True), west_of(be, True)
        coef = [[], [], [], [], []]
        for b in range(NB):
            a_s, b_s = pltpu.roll(an[b], 1, 0), pltpu.roll(bn[b], 1, 0)
            c0 = keep[b] - (ae[b] - bw[b]) - (an[b] - b_s)
            for n, val in enumerate((c0, -be[b], aw[b], -bn[b], a_s)):
                coef[n].append(val)
                coefs[n, b, z] = val

        def put(b, r, j, val):
            first[b, r, z] = val

        stencil(
            lambda b, r, zz: q_v[r, zz, :, col(b)], coef, z, [mix[b] for b in range(NB)], put,
        )

    zero = jnp.zeros((NY, L), F32)

    def chunk(i, carry):
        @pl.when(i < NC - 1)
        def _():
            for cp in fetch(jnp.minimum(i + 1, NC - 1)):
                cp.wait()

        def body(h, _):
            level(i * CH + h)
            return 0

        lax.fori_loop(0, CH, body, 0, unroll=UNROLL1)
        for cp in store(i):
            cp.start()
        he, hw = carry
        for r in range(NR):
            acc_e, acc_w = zero, zero
            for h in range(CH):
                acc_e = to_lane(acc_e, first[NB - 1, r, i * CH + h], h, L - 1)
                acc_w = to_lane(acc_w, first[0, r, i * CH + h], h, 0)
            he = he + pltpu.roll(acc_e, r * NZ + i * CH, 1)
            hw = hw + pltpu.roll(acc_w, r * NZ + i * CH, 1)
        return he, hw

    cols[0], cols[1] = lax.fori_loop(0, NC, chunk, (zero, zero))
    ff = first.reshape(NB * NQ * NY, L)
    for b in range(NB):
        for g in range(0, NQ, 8):
            at = (b * NQ + g) * NY
            rows[0, b, g : g + 8, :] = ff[pl.ds(at + NY - 1, 8, stride=NY), :]
            rows[1, b, g : g + 8, :] = ff[pl.ds(at, 8, stride=NY), :]
    for i in range(NC):
        for cp in store(i):
            cp.wait()


def spread3(x):
    x = jnp.where(lanes() < NZ, x, 0.0)
    return x + pltpu.roll(x, NZ, 1) + pltpu.roll(x, 2 * NZ, 1)


def face(w_a, w_b, k_a, k_b, u):
    p = w_a * w_b
    d = 0.5 * (k_a + k_b) * p
    s = u * p
    return spread3(jnp.maximum(s, 0.0) + d), spread3(jnp.minimum(s, 0.0) - d)


def remap_kernel(
    idx, src, live, coup, got, tiles_h, wet, hown, rows_in, cols, edge_n, edge_s, r1, r2,
    forcing, ns1, ns2, ew1, ew2, hnew, facec, fluxes1, rows, facey, fluxy,
    tiles, sem,
):
    def fetch(i):
        at = pl.ds(i * NB, NB)
        return pltpu.make_async_copy(tiles_h.at[at], tiles.at[at], sem.at[i])

    for i in range(NY):
        fetch(i).start()
    row = subl()
    zero = jnp.zeros((NY, L), F32)
    cvec = []
    for r in range(NR):
        c = zero
        for f in range(10):
            c = jnp.where(row == f, coup[r, f], c)
        cvec.append(c)

    def target_row(i, _):
        fetch(i).wait()
        for s in range(NB):
            t = i * NB + s
            n = live[t]
            parts = []
            for k in range(4):
                p = src[k, t]
                blk = got[p // 6 * 8 + p % 6]
                parts.append(jnp.where(k < n, blk, jnp.zeros_like(blk)))
            acc = jnp.dot(jnp.concatenate(parts, axis=1), tiles[t], preferred_element_type=F32)
            for r in range(NR):
                forcing[s, r, pl.ds(i, 1), :] = jnp.sum(acc * cvec[r], axis=0, keepdims=True)
        return 0

    lax.fori_loop(0, NY, target_row, 0, unroll=4)
    for s in range(NB):
        w = wet[:, col(s)].astype(F32)
        for r in range(NR):
            forcing[s, r] = forcing[s, r] * w
    l_east, l_west = idx[2], idx[3]
    oe0, oe1, ow0, ow1 = hown[0], hown[1], hown[2], hown[3]
    ge0, ge1 = got[l_east * 8 + 6].astype(F32), got[l_east * 8 + 7].astype(F32)
    gw0, gw1 = got[l_west * 8 + 6].astype(F32), got[l_west * 8 + 7].astype(F32)

    def wcol(x):
        return jnp.broadcast_to(x[:, NQ : NQ + 1], (NY, L))

    ae, be = face(wcol(oe0), wcol(ge0), oe1, ge1, pltpu.roll(oe1, L - NZ, 1))
    aw, bw = face(wcol(gw0), wcol(ow0), gw1, ow1, pltpu.roll(gw1, L - NZ, 1))
    facec[0], facec[1], facec[2], facec[3] = ae, be, aw, bw
    fe = ae * oe0 + be * ge0
    fw = aw * gw0 + bw * ow0
    fluxes1[0], fluxes1[1] = fe, fw
    lane = lanes()
    for b in range(NB):
        hn_w, hs_w = from_sides(idx, r1, r2, (b, slice(192, 208)))
        pn = edge_n[b, 200:208, :] * hn_w[8:16]
        ps = hs_w[8:16] * edge_s[b, 200:208, :]
        fluxy[0, b, 120:128, :] = jnp.zeros((8, L), F32)
        fluxy[1, b, 120:128, :] = jnp.zeros((8, L), F32)
        halves = {}

        def halo(at):
            g = at // 16 * 16
            if g not in halves:
                halves[g] = from_sides(idx, r1, r2, (b, slice(g, g + 16)))
            n, s = halves[g]
            return n[at - g : at - g + 8], s[at - g : at - g + 8]

        for g in range(0, NZ, 8):
            kk, nn = slice(NQ + g, NQ + g + 8), slice(NQ + NZ + g, NQ + NZ + g + 8)
            kn, ks = halo(NQ + g)
            _, sn = halo(NQ + NZ + g)
            d, u = 0.5 * (edge_n[b, kk, :] + kn) * pn, edge_n[b, nn, :] * pn
            a_n, b_n = jnp.maximum(u, 0.0) + d, jnp.minimum(u, 0.0) - d
            d, u = 0.5 * (ks + edge_s[b, kk, :]) * ps, sn * ps
            a_s, b_s = jnp.maximum(u, 0.0) + d, jnp.minimum(u, 0.0) - d
            for n, val in enumerate((a_n, b_n, a_s, b_s)):
                facey[n, b, g : g + 8, :] = val
            for r in range(NR):
                j = r * NZ + g
                qn, qs = halo(j)
                fluxy[0, b, j : j + 8, :] = a_n * edge_n[b, j : j + 8, :] + b_n * qn
                fluxy[1, b, j : j + 8, :] = a_s * qs + b_s * edge_s[b, j : j + 8, :]
    he, hw = cols[0] - fe, cols[1] + fw
    for side, y, sign in ((0, NY - 1, -1.0), (1, 0, 1.0)):
        he = he + jnp.where(row == y, sign * fluxy[side, NB - 1].T[L - 1 : L, :], 0.0)
        hw = hw + jnp.where(row == y, sign * fluxy[side, 0].T[0:1, :], 0.0)
    for r in range(NR):
        here = lane == r * NZ
        he = he + jnp.where(here, pltpu.roll(forcing[4, r], r * NZ + 1, 1), 0.0)
        hw = hw + jnp.where(here, pltpu.roll(forcing[0, r], r * NZ, 1), 0.0)
    hnew[0], hnew[1] = he, hw
    leven = idx[1] == 1
    ew1[...] = jnp.where(leven, he, hw).astype(BF)
    ew2[...] = jnp.where(leven, hw, he).astype(BF)
    fill = jnp.zeros((L - NY, L), F32)
    fet = jnp.concatenate([fe, fill], axis=0).T
    fwt = jnp.concatenate([fw, fill], axis=0).T
    even = idx[0] == 1
    big = lanes(L)
    sub = subl(L)
    for b in range(NB):
        edges = []
        for side, y in ((0, NY - 1), (1, 0)):
            v = rows_in[side, b] + (fluxy[1, b] if side else -fluxy[0, b])
            for r in range(NR):
                v = v + jnp.where(sub == r * NZ, jnp.broadcast_to(forcing[b, r, y : y + 1, :], (L, L)), 0.0)
            if b == NB - 1:
                v = v - jnp.where(big == L - 1, jnp.broadcast_to(fet[:, y : y + 1], (L, L)), 0.0)
            if b == 0:
                v = v + jnp.where(big == 0, jnp.broadcast_to(fwt[:, y : y + 1], (L, L)), 0.0)
            rows[side, b] = v
            edges.append(v)
        n, s = edges
        ns1[b] = jnp.where(even, n, s).astype(BF)
        ns2[b] = jnp.where(even, s, n).astype(BF)


def step2_kernel(
    idx, r1, r2, g1, g2, wet, forcing, hnew, facec, fluxes1, rows, facey, fluxy, coefs, first_h,
    out_h,
    over_n, over_s, first, out_v, dl, mix, sem, osem,
):
    def copy(i, b):
        zs = pl.ds(i * CH, CH)
        return pltpu.make_async_copy(out_v.at[b, :, zs], out_h.at[:, zs, :, pl.ds(b * L, L)], osem.at[i, b])

    def fetch(i):
        zs = pl.ds(i * CH, CH)
        return pltpu.make_async_copy(first_h.at[:, :, zs], first.at[:, :, zs], sem.at[i])

    for i in range(NC):
        fetch(i).start()
    for b in range(NB):
        for g in range(0, NQ, 8):
            if g % 16 == 0:
                pair = from_sides(idx, r1, r2, (b, slice(g, g + 16)))
            hn, hs = pair[0][g % 16 : g % 16 + 8], pair[1][g % 16 : g % 16 + 8]
            a_n, b_n, a_s, b_s = (facey[n, b, g % NZ : g % NZ + 8, :] for n in range(4))
            over_n[b, g : g + 8, :] = a_n * rows[0, b, g : g + 8, :] + b_n * hn
            over_s[b, g : g + 8, :] = a_s * hs + b_s * rows[1, b, g : g + 8, :]
    leven = idx[1] == 1
    a, c = g1[...].astype(F32), g2[...].astype(F32)
    from_e, from_w = jnp.where(leven, a, c), jnp.where(leven, c, a)
    dl[0] = facec[0] * hnew[0] + facec[1] * from_e
    dl[1] = facec[2] * from_w + facec[3] * hnew[1]
    for b in range(NB):
        mix[b] = VMIX * wet[:, col(b)].astype(F32)
    lane = lanes()

    def ready(i):
        fetch(i).wait()
        for r in range(NR):
            back = L - (r * NZ + i * CH)
            over_e, over_w = pltpu.roll(fluxes1[0], back, 1), pltpu.roll(fluxes1[1], back, 1)
            for h in range(CH):
                z = i * CH + h
                at = pl.ds(r * NZ + z, 1)
                for b in range(NB):
                    v = add_rows(first[b, r, z], fluxy[1, b, at, :], fluxy[0, b, at, :])
                    if b == 0:
                        v = v + jnp.where(lane == 0, pltpu.roll(over_w, (L - h) % L, 1), 0.0)
                    if b == NB - 1:
                        v = v - jnp.where(lane == L - 1, pltpu.roll(over_e, L - 1 - h, 1), 0.0)
                    first[b, r, z] = v

    ready(0)
    for b in range(NB):
        for r in range(NR):
            first[b, r, 0] = first[b, r, 0] + forcing[b, r]

    def level(h, z, over_e, over_w):
        coef = [[coefs[n, b, z] for b in range(NB)] for n in range(5)]

        def put(b, r, j, val):
            if b == 0:
                val = val + jnp.where(lane == 0, pltpu.roll(over_w[r], (L - h) % L, 1), 0.0)
            if b == NB - 1:
                val = val - jnp.where(lane == L - 1, pltpu.roll(over_e[r], L - 1 - h, 1), 0.0)
            at = pl.ds(j, 1)
            out_v[b, r, z] = add_rows(val, over_s[b, at, :], over_n[b, at, :])

        stencil(lambda b, r, zz: first[b, r, zz], coef, z, [mix[b] for b in range(NB)], put)

    def chunk(i, _):
        @pl.when(i < NC - 1)
        def _():
            ready(jnp.minimum(i + 1, NC - 1))

        over_e = [pltpu.roll(dl[0], L - (r * NZ + i * CH), 1) for r in range(NR)]
        over_w = [pltpu.roll(dl[1], L - (r * NZ + i * CH), 1) for r in range(NR)]
        for h in range(CH):
            level(h, i * CH + h, over_e, over_w)

        @pl.when(i == 0)
        def _():
            for b in range(NB):
                for r in range(NR):
                    out_v[b, r, 0] = out_v[b, r, 0] + forcing[b, r]

        for b in range(NB):
            copy(i, b).start()
        return 0

    lax.fori_loop(0, NC, chunk, 0)
    for i in range(NC):
        for b in range(NB):
            copy(i, b).wait()


def vmem(x):
    return pltpu.with_memory_space_constraint(x, pltpu.VMEM)


def hbm(x):
    return pltpu.with_memory_space_constraint(x, pltpu.HBM)


def shards(
    fluxes, tracers, diffusivity, east_speed, north_speed, wet, coupling, sources, live_slots, tiles
):
    sds = jax.ShapeDtypeStruct
    band, lon = lax.axis_index("comp"), lax.axis_index("lon")
    n_lon = lax.axis_size("lon")
    idx = jnp.stack([1 - band % 2, 1 - lon % 2, (lon + 1) % n_lon, (lon + n_lon - 1) % n_lon]).astype(jnp.int32)
    dma = pltpu.SemaphoreType.DMA
    q5, s5 = (NB, NR, NZ, NY, L), (NB, NZ, NY, L)
    cf = (5, NB, NZ, NY, L)
    nat, nats, tile = (NR, NZ, NY, 640), (NZ, NY, 640), (NB, NY, L)
    rowpay, edgepay = (NB, 208, L), (NB, 128, L)

    def params(mib):
        return pltpu.CompilerParams(vmem_limit_bytes=mib << 20)

    def cost(us):
        return pl.CostEstimate(flops=0, transcendentals=0, bytes_accessed=us * 3_000_000)

    flux, q, k, e, n, wh = map(
        hbm, (fluxes[:, 0, :], tracers, diffusivity, east_speed, north_speed, wet)
    )
    a2a, ns1, ns2, hown, edge_n, edge_s = pl.pallas_call(
        pack_kernel,
        out_shape=(
            sds((16, 8, NY, L), BF), sds(rowpay, BF), sds(rowpay, BF), sds((4, NY, L), F32),
            sds(rowpay, F32), sds(rowpay, F32),
        ),
        in_specs=[SM] + [ANY] * 6,
        out_specs=(VM,) * 6,
        scratch_shapes=[
            pltpu.VMEM((10, 12288), BF), pltpu.VMEM(q5, F32), pltpu.VMEM(s5, F32), pltpu.VMEM(s5, F32),
            pltpu.VMEM((NZ, NY, L), F32), pltpu.VMEM((NY, 640), jnp.int32), dma((18,)),
        ],
        cost_estimate=cost(6),
        compiler_params=params(20),
        name="pack",
    )(idx, flux, q, k, e, n, wh)
    swap_a = [(i, i ^ 1) for i in range(8)]
    swap_b = [(i, i + 1) for i in (1, 3, 5)] + [(i + 1, i) for i in (1, 3, 5)]
    r1 = lax.ppermute(ns1, "comp", swap_a)
    r2 = lax.ppermute(ns2, "comp", swap_b)
    got = lax.all_to_all(a2a, "lon", split_axis=0, concat_axis=0, tiled=True)
    first, coefs, rows, cols = pl.pallas_call(
        step1_kernel,
        out_shape=(pltpu.HBM(q5, F32), pltpu.HBM(cf, F32), sds((2,) + edgepay, F32), sds((2, NY, L), F32)),
        in_specs=[ANY] * 5,
        out_specs=(ANY,) * 2 + (VM,) * 2,
        scratch_shapes=[
            pltpu.VMEM(nat, F32), pltpu.VMEM(nats, F32), pltpu.VMEM(nats, F32), pltpu.VMEM(nats, F32),
            pltpu.VMEM(q5, F32), pltpu.VMEM(cf, F32),
            pltpu.VMEM((NY, 640), jnp.int32),
            pltpu.VMEM(tile, F32), pltpu.VMEM(tile, F32), pltpu.VMEM(tile, F32), pltpu.VMEM(tile, F32),
            dma((NC + 1, 4)), dma((NC, 2)),
        ],
        cost_estimate=cost(30),
        compiler_params=params(28),
        name="step1",
    )(wh, q, k, e, n)
    forcing, ms1, ms2, ew1, ew2, hnew, facec, fluxes1, rows, facey, fluxy = pl.pallas_call(
        remap_kernel,
        out_shape=(
            sds((NB, NR, NY, L), F32), sds(edgepay, BF), sds(edgepay, BF), sds((NY, L), BF), sds((NY, L), BF),
            sds((2, NY, L), F32), sds((4, NY, L), F32), sds((2, NY, L), F32),
            sds((2,) + edgepay, F32), sds((4, NB, NZ, L), F32), sds((2,) + edgepay, F32),
        ),
        in_specs=[SM] * 4 + [VM, ANY] + [VM] * 8,
        out_specs=(VM,) * 11,
        scratch_shapes=[pltpu.VMEM((80, 512, L), BF), dma((NY,))],
        cost_estimate=cost(7),
        compiler_params=params(20),
        name="remap",
    )(idx, sources.T, live_slots, coupling, got.reshape(128, NY, L), hbm(tiles.reshape(80, 512, L)), wet, hown, rows, cols,
      edge_n, edge_s, r1, r2)
    lon_a = [(i, i ^ 1) for i in range(16)]
    lon_b = [((2 * i + 1) % 16, (2 * i + 2) % 16) for i in range(8)]
    lon_b = lon_b + [(b, a) for a, b in lon_b]
    r1 = lax.ppermute(ms1, "comp", swap_a)
    r2 = lax.ppermute(ms2, "comp", swap_b)
    g1 = lax.ppermute(ew1, "lon", lon_a)
    g2 = lax.ppermute(ew2, "lon", lon_b)
    return pl.pallas_call(
        step2_kernel,
        out_shape=sds(tracers.shape, F32),
        in_specs=[SM] + [VM] * 13 + [ANY],
        out_specs=ANY,
        scratch_shapes=[
            pltpu.VMEM(edgepay, F32), pltpu.VMEM(edgepay, F32), pltpu.VMEM(q5, F32), pltpu.VMEM(q5, F32),
            pltpu.VMEM((2, NY, L), F32), pltpu.VMEM(tile, F32), dma((NC,)), dma((NC, NB)),
        ],
        cost_estimate=cost(7),
        compiler_params=params(14),
        name="step2",
    )(idx, r1, r2, g1, g2, wet, forcing, hnew, facec, fluxes1, rows, facey, fluxy, vmem(coefs), hbm(first))


def solution(mesh):
    return jax.shard_map(
        shards,
        mesh=mesh,
        in_specs=(
            P(None, ("comp", "lon"), None),
            P(None, None, "comp", "lon"),
            P(None, "comp", "lon"),
            P(None, "comp", "lon"),
            P(None, "comp", "lon"),
            P("comp", "lon"),
            P(),
            P(("comp", "lon"), None),
            P(("comp", "lon")),
            P(("comp", "lon"), None, None, None),
        ),
        out_specs=P(None, None, "comp", "lon"),
        check_vma=False,
    )
```

```python
import functools

import jax
import jax.numpy as jnp
from jax import lax
from jax.experimental import pallas as pl
from jax.experimental.pallas import tpu as pltpu
from jax.sharding import PartitionSpec as P

VMIX = 0.2
L = 128
F32 = jnp.float32
BF = jnp.bfloat16
ANY = pl.BlockSpec(memory_space=pltpu.HBM)
VM = pl.BlockSpec(memory_space=pltpu.VMEM)
SM = pl.BlockSpec(memory_space=pltpu.SMEM)
NB, NR, NZ, NY = 5, 3, 40, 16
NQ = NR * NZ
CH = 8
NC = NZ // CH
C1 = 4
N1 = NZ // C1


def lanes(rows=NY):
    return lax.broadcasted_iota(jnp.int32, (rows, L), 1)


def subl(rows=NY):
    return lax.broadcasted_iota(jnp.int32, (rows, L), 0)


def col(b):
    return slice(b * L, (b + 1) * L)


def east_of(vals):
    rolled = [pltpu.roll(v, L - 1, 1) for v in vals]
    last = lanes() == L - 1
    return [jnp.where(last, rolled[b + 1], rolled[b]) if b < NB - 1 else rolled[b] for b in range(NB)]


def west_of(vals, wrap=False):
    rolled = [pltpu.roll(v, 1, 1) for v in vals]
    head = lanes() == 0
    return [jnp.where(head, rolled[b - 1], rolled[b]) if b or wrap else rolled[b] for b in range(NB)]


def to_lane(acc, val, h, source):
    return jnp.where(lanes() == h, pltpu.roll(val, (h - source) % L, 1), acc)


def pack_kernel(
    idx, flux_h, q_h, k_h, e_h, n_h, wet_h,
    a2a, ns1, ns2, hown, edge_n, edge_s,
    flux, q_v, k_v, n_v, e_v, wet_i, sem,
):
    first_two = [pltpu.make_async_copy(flux_h, flux, sem.at[0]), pltpu.make_async_copy(wet_h, wet_i, sem.at[1])]
    last_e = pltpu.make_async_copy(e_h.at[:, :, pl.ds(4 * L, L)], e_v, sem.at[2])
    copies = {}
    for b in range(NB):
        at = pl.ds(b * L, L)
        copies[b] = [
            pltpu.make_async_copy(q_h.at[:, :, :, at], q_v.at[b], sem.at[3 + 3 * b]),
            pltpu.make_async_copy(k_h.at[:, :, at], k_v.at[b], sem.at[4 + 3 * b]),
            pltpu.make_async_copy(n_h.at[:, pl.ds(8, 8), at], n_v.at[b], sem.at[5 + 3 * b]),
        ]
    for cp in first_two:
        cp.start()
    order = (4, 0, 1, 2, 3)
    for b in order:
        for cp in copies[b]:
            cp.start()
        if b == 4:
            last_e.start()
    for cp in first_two:
        cp.wait()
    pad = jnp.zeros((6, L), BF)
    for d in range(16):
        for m in range(6):
            a2a[d, m] = jnp.concatenate([flux[:, col(d * 6 + m)], pad], axis=0)
    for b in (4, 0):
        for cp in copies[b]:
            cp.wait()
    last_e.wait()
    lane = lanes()
    zero = jnp.zeros((NY, L), F32)

    def edge(i, carry):
        e0, e1, w0, w1 = carry
        acc = [zero] * 9
        for h in range(CH):
            z = i * CH + h
            for r in range(NR):
                acc[r] = to_lane(acc[r], q_v[4, r, z], h, L - 1)
                acc[3 + r] = to_lane(acc[3 + r], q_v[0, r, z], h, 0)
            acc[6] = to_lane(acc[6], k_v[4, z], h, L - 1)
            acc[7] = to_lane(acc[7], e_v[z], h, L - 1)
            acc[8] = to_lane(acc[8], k_v[0, z], h, 0)
        for r in range(NR):
            e0 = e0 + pltpu.roll(acc[r], r * NZ + i * CH, 1)
            w0 = w0 + pltpu.roll(acc[3 + r], r * NZ + i * CH, 1)
        e1 = e1 + pltpu.roll(acc[6], i * CH, 1) + pltpu.roll(acc[7], NZ + i * CH, 1)
        w1 = w1 + pltpu.roll(acc[8], i * CH, 1)
        return e0, e1, w0, w1

    e0, e1, w0, w1 = lax.fori_loop(0, NC, edge, (zero, zero, zero, zero))
    e0 = jnp.where(lane == NQ, pltpu.roll(wet_i[:, col(4)].astype(F32), NQ + 1, 1), e0)
    w0 = jnp.where(lane == NQ, pltpu.roll(wet_i[:, col(0)].astype(F32), NQ, 1), w0)
    hown[0], hown[1], hown[2], hown[3] = e0, e1, w0, w1
    l_east, l_west = idx[2], idx[3]
    a2a[l_east, 6] = e0.astype(BF)
    a2a[l_east, 7] = e1.astype(BF)
    a2a[l_west, 6] = w0.astype(BF)
    a2a[l_west, 7] = w1.astype(BF)
    even = idx[0] == 1
    for b in order:
        if b not in (4, 0):
            for cp in copies[b]:
                cp.wait()
        for ref, count, base in ((q_v, NQ, 0), (k_v, NZ, NQ)):
            flat = ref.reshape(NB * count * NY, L)
            for g in range(0, count, 8):
                at = (b * count + g) * NY
                edge_n[b, base + g : base + g + 8, :] = flat[pl.ds(at + NY - 1, 8, stride=NY), :]
                edge_s[b, base + g : base + g + 8, :] = flat[pl.ds(at, 8, stride=NY), :]
        flat = n_v.reshape(NB * NZ * 8, L)
        for g in range(0, NZ, 8):
            top = flat[pl.ds((b * NZ + g) * 8 + 7, 8, stride=8), :]
            edge_n[b, NQ + NZ + g : NQ + NZ + g + 8, :] = top
            edge_s[b, NQ + NZ + g : NQ + NZ + g + 8, :] = top
        w = wet_i[:, col(b)].astype(F32)
        edge_n[b, 200:208, :] = jnp.broadcast_to(w[NY - 1 : NY, :], (8, L))
        edge_s[b, 200:208, :] = jnp.broadcast_to(w[0:1, :], (8, L))
        for g in range(0, 208, 16):
            n, s = edge_n[b, g : g + 16, :], edge_s[b, g : g + 16, :]
            ns1[b, g : g + 16, :] = jnp.where(even, n, s).astype(BF)
            ns2[b, g : g + 16, :] = jnp.where(even, s, n).astype(BF)


def stencil(get, coef, z, mix, put):
    zu, zd = jnp.maximum(z - 1, 0), jnp.minimum(z + 1, NZ - 1)
    c0, ce, cw, cn, cs = coef
    for r in range(NR):
        q = [get(b, r, z) for b in range(NB)]
        qe, qw = east_of(q), west_of(q)
        j = r * NZ + z
        for b in range(NB):
            qn, qs = pltpu.roll(q[b], NY - 1, 0), pltpu.roll(q[b], 1, 0)
            out = c0[b] * q[b] + ce[b] * qe[b] + cw[b] * qw[b] + cn[b] * qn + cs[b] * qs
            put(b, r, j, out + mix[b] * (get(b, r, zu) + get(b, r, zd)))


def from_sides(idx, r1, r2, at):
    even = idx[0] == 1
    a, c = r1[at].astype(F32), r2[at].astype(F32)
    return jnp.where(even, a, c), jnp.where(even, c, a)


def add_rows(val, south, north):
    sub = subl(8)
    low = val[0:8] + jnp.where(sub == 0, jnp.broadcast_to(south, (8, L)), 0.0)
    high = val[8:16] - jnp.where(sub == 7, jnp.broadcast_to(north, (8, L)), 0.0)
    return jnp.concatenate([low, high], axis=0)


def step1_kernel(
    wet_h, q_h, k_h, e_h, n_h,
    first_h, coefs_h, rows, cols,
    q_v, k_v, e_v, n_v, first, coefs, wet_i, pe, pn, keep, mix, sem, osem,
):
    cw = pltpu.make_async_copy(wet_h, wet_i, sem.at[N1, 0])
    cw.start()

    def fetch(i):
        zs = pl.ds(i * C1, C1)
        return [
            pltpu.make_async_copy(q_h.at[:, zs], q_v.at[:, zs], sem.at[i, 0]),
            pltpu.make_async_copy(k_h.at[zs], k_v.at[zs], sem.at[i, 1]),
            pltpu.make_async_copy(e_h.at[zs], e_v.at[zs], sem.at[i, 2]),
            pltpu.make_async_copy(n_h.at[zs], n_v.at[zs], sem.at[i, 3]),
        ]

    def store(i):
        zs = pl.ds(i * C1, C1)
        return [
            pltpu.make_async_copy(first.at[:, :, zs], first_h.at[:, :, zs], osem.at[i, 0]),
            pltpu.make_async_copy(coefs.at[:, :, zs], coefs_h.at[:, :, zs], osem.at[i, 1]),
        ]

    for i in range(N1):
        for cp in fetch(i):
            cp.start()
    cw.wait()
    row, lane = subl(), lanes()
    w = [wet_i[:, col(b)].astype(F32) for b in range(NB)]
    we = east_of(w)
    for b in range(NB):
        p = w[b] * we[b]
        pe[b] = 0.5 * (jnp.where(lane == L - 1, 0.0, p) if b == NB - 1 else p)
        pn[b] = 0.5 * w[b] * jnp.where(row == NY - 1, 0.0, pltpu.roll(w[b], NY - 1, 0))
        mix[b] = VMIX * w[b]
        keep[b] = 1.0 - 2.0 * VMIX * w[b]
    for cp in fetch(0):
        cp.wait()

    def level(z):
        k = [k_v[z, :, col(b)] for b in range(NB)]
        ke = east_of(k)
        ae, be, an, bn = [], [], [], []
        for b in range(NB):
            kn = pltpu.roll(k[b], NY - 1, 0)
            d = (k[b] + ke[b]) * pe[b]
            u = 2.0 * e_v[z, :, col(b)] * pe[b]
            ae.append(jnp.maximum(u, 0.0) + d)
            be.append(jnp.minimum(u, 0.0) - d)
            d = (k[b] + kn) * pn[b]
            u = 2.0 * n_v[z, :, col(b)] * pn[b]
            an.append(jnp.maximum(u, 0.0) + d)
            bn.append(jnp.minimum(u, 0.0) - d)
        aw, bw = west_of(ae, True), west_of(be, True)
        coef = [[], [], [], [], []]
        for b in range(NB):
            a_s, b_s = pltpu.roll(an[b], 1, 0), pltpu.roll(bn[b], 1, 0)
            c0 = keep[b] - (ae[b] - bw[b]) - (an[b] - b_s)
            for n, val in enumerate((c0, -be[b], aw[b], -bn[b], a_s)):
                coef[n].append(val)
                coefs[n, b, z] = val

        def put(b, r, j, val):
            first[b, r, z] = val

        stencil(
            lambda b, r, zz: q_v[r, zz, :, col(b)], coef, z, [mix[b] for b in range(NB)], put,
        )

    zero = jnp.zeros((NY, L), F32)

    def chunk(i, _):
        @pl.when(i < N1 - 1)
        def _():
            for cp in fetch(jnp.minimum(i + 1, N1 - 1)):
                cp.wait()

        def body(h, _):
            level(i * C1 + h)
            return 0

        lax.fori_loop(0, C1, body, 0, unroll=4)
        for cp in store(i):
            cp.start()
        return 0

    lax.fori_loop(0, N1, chunk, 0)

    def edge(i, carry):
        he, hw = carry
        for r in range(NR):
            acc_e, acc_w = zero, zero
            for h in range(CH):
                acc_e = to_lane(acc_e, first[NB - 1, r, i * CH + h], h, L - 1)
                acc_w = to_lane(acc_w, first[0, r, i * CH + h], h, 0)
            he = he + pltpu.roll(acc_e, r * NZ + i * CH, 1)
            hw = hw + pltpu.roll(acc_w, r * NZ + i * CH, 1)
        return he, hw

    cols[0], cols[1] = lax.fori_loop(0, NC, edge, (zero, zero))
    ff = first.reshape(NB * NQ * NY, L)
    for b in range(NB):
        for g in range(0, NQ, 8):
            at = (b * NQ + g) * NY
            rows[0, b, g : g + 8, :] = ff[pl.ds(at + NY - 1, 8, stride=NY), :]
            rows[1, b, g : g + 8, :] = ff[pl.ds(at, 8, stride=NY), :]
    for i in range(N1):
        for cp in store(i):
            cp.wait()


def spread3(x):
    x = jnp.where(lanes() < NZ, x, 0.0)
    return x + pltpu.roll(x, NZ, 1) + pltpu.roll(x, 2 * NZ, 1)


def face(w_a, w_b, k_a, k_b, u):
    p = w_a * w_b
    d = 0.5 * (k_a + k_b) * p
    s = u * p
    return spread3(jnp.maximum(s, 0.0) + d), spread3(jnp.minimum(s, 0.0) - d)


def remap_kernel(
    idx, src, live, coup, got, tiles_h, wet, hown, rows_in, cols, edge_n, edge_s, r1, r2,
    forcing, ns1, ns2, ew1, ew2, hnew, facec, fluxes1, rows, facey, fluxy,
    tiles, sem,
):
    def fetch(i):
        at = pl.ds(i * NB, NB)
        return pltpu.make_async_copy(tiles_h.at[at], tiles.at[at], sem.at[i])

    for i in range(NY):
        fetch(i).start()
    row = subl()
    zero = jnp.zeros((NY, L), F32)
    l_east, l_west = idx[2], idx[3]
    oe0, oe1, ow0, ow1 = hown[0], hown[1], hown[2], hown[3]
    ge0, ge1 = got[l_east * 8 + 6].astype(F32), got[l_east * 8 + 7].astype(F32)
    gw0, gw1 = got[l_west * 8 + 6].astype(F32), got[l_west * 8 + 7].astype(F32)

    def wcol(x):
        return jnp.broadcast_to(x[:, NQ : NQ + 1], (NY, L))

    ae, be = face(wcol(oe0), wcol(ge0), oe1, ge1, pltpu.roll(oe1, L - NZ, 1))
    aw, bw = face(wcol(gw0), wcol(ow0), gw1, ow1, pltpu.roll(gw1, L - NZ, 1))
    facec[0], facec[1], facec[2], facec[3] = ae, be, aw, bw
    fe = ae * oe0 + be * ge0
    fw = aw * gw0 + bw * ow0
    fluxes1[0], fluxes1[1] = fe, fw
    lane = lanes()
    for b in range(NB):
        hn_w, hs_w = from_sides(idx, r1, r2, (b, slice(192, 208)))
        pn = edge_n[b, 200:208, :] * hn_w[8:16]
        ps = hs_w[8:16] * edge_s[b, 200:208, :]
        fluxy[0, b, 120:128, :] = jnp.zeros((8, L), F32)
        fluxy[1, b, 120:128, :] = jnp.zeros((8, L), F32)
        halves = {}

        def halo(at):
            g = at // 16 * 16
            if g not in halves:
                halves[g] = from_sides(idx, r1, r2, (b, slice(g, g + 16)))
            n, s = halves[g]
            return n[at - g : at - g + 8], s[at - g : at - g + 8]

        for g in range(0, NZ, 8):
            kk, nn = slice(NQ + g, NQ + g + 8), slice(NQ + NZ + g, NQ + NZ + g + 8)
            kn, ks = halo(NQ + g)
            _, sn = halo(NQ + NZ + g)
            d, u = 0.5 * (edge_n[b, kk, :] + kn) * pn, edge_n[b, nn, :] * pn
            a_n, b_n = jnp.maximum(u, 0.0) + d, jnp.minimum(u, 0.0) - d
            d, u = 0.5 * (ks + edge_s[b, kk, :]) * ps, sn * ps
            a_s, b_s = jnp.maximum(u, 0.0) + d, jnp.minimum(u, 0.0) - d
            for n, val in enumerate((a_n, b_n, a_s, b_s)):
                facey[n, b, g : g + 8, :] = val
            for r in range(NR):
                j = r * NZ + g
                qn, qs = halo(j)
                fluxy[0, b, j : j + 8, :] = a_n * edge_n[b, j : j + 8, :] + b_n * qn
                fluxy[1, b, j : j + 8, :] = a_s * qs + b_s * edge_s[b, j : j + 8, :]
    cvec = []
    for r in range(NR):
        c = zero
        for f in range(10):
            c = jnp.where(row == f, coup[r, f], c)
        cvec.append(c)

    def target_row(i, _):
        fetch(i).wait()
        for s in range(NB):
            t = i * NB + s
            n = live[t]
            parts = []
            for k in range(4):
                p = src[k, t]
                blk = got[p // 6 * 8 + p % 6]
                parts.append(jnp.where(k < n, blk, jnp.zeros_like(blk)))
            acc = jnp.dot(jnp.concatenate(parts, axis=1), tiles[t], preferred_element_type=F32)
            for r in range(NR):
                forcing[s, r, pl.ds(i, 1), :] = jnp.sum(acc * cvec[r], axis=0, keepdims=True)
        return 0

    lax.fori_loop(0, NY, target_row, 0, unroll=4)
    for s in range(NB):
        w = wet[:, col(s)].astype(F32)
        for r in range(NR):
            forcing[s, r] = forcing[s, r] * w
    he, hw = cols[0] - fe, cols[1] + fw
    for side, y, sign in ((0, NY - 1, -1.0), (1, 0, 1.0)):
        he = he + jnp.where(row == y, sign * fluxy[side, NB - 1].T[L - 1 : L, :], 0.0)
        hw = hw + jnp.where(row == y, sign * fluxy[side, 0].T[0:1, :], 0.0)
    for r in range(NR):
        here = lane == r * NZ
        he = he + jnp.where(here, pltpu.roll(forcing[4, r], r * NZ + 1, 1), 0.0)
        hw = hw + jnp.where(here, pltpu.roll(forcing[0, r], r * NZ, 1), 0.0)
    hnew[0], hnew[1] = he, hw
    leven = idx[1] == 1
    ew1[...] = jnp.where(leven, he, hw).astype(BF)
    ew2[...] = jnp.where(leven, hw, he).astype(BF)
    fill = jnp.zeros((L - NY, L), F32)
    fet = jnp.concatenate([fe, fill], axis=0).T
    fwt = jnp.concatenate([fw, fill], axis=0).T
    even = idx[0] == 1
    big = lanes(L)
    sub = subl(L)
    for b in range(NB):
        edges = []
        for side, y in ((0, NY - 1), (1, 0)):
            v = rows_in[side, b] + (fluxy[1, b] if side else -fluxy[0, b])
            for r in range(NR):
                v = v + jnp.where(sub == r * NZ, jnp.broadcast_to(forcing[b, r, y : y + 1, :], (L, L)), 0.0)
            if b == NB - 1:
                v = v - jnp.where(big == L - 1, jnp.broadcast_to(fet[:, y : y + 1], (L, L)), 0.0)
            if b == 0:
                v = v + jnp.where(big == 0, jnp.broadcast_to(fwt[:, y : y + 1], (L, L)), 0.0)
            rows[side, b] = v
            edges.append(v)
        n, s = edges
        ns1[b] = jnp.where(even, n, s).astype(BF)
        ns2[b] = jnp.where(even, s, n).astype(BF)


def step2_kernel(
    idx, r1, r2, g1, g2, wet, forcing, hnew, facec, fluxes1, rows, facey, fluxy, coefs, first_in,
    out_h,
    over_n, over_s, first, out_v, dl, mix, osem,
):
    def copy(i, b):
        zs = pl.ds(i * CH, CH)
        return pltpu.make_async_copy(out_v.at[b, :, zs], out_h.at[:, zs, :, pl.ds(b * L, L)], osem.at[i, b])

    for b in range(NB):
        for g in range(0, NQ, 8):
            if g % 16 == 0:
                pair = from_sides(idx, r1, r2, (b, slice(g, g + 16)))
            hn, hs = pair[0][g % 16 : g % 16 + 8], pair[1][g % 16 : g % 16 + 8]
            a_n, b_n, a_s, b_s = (facey[n, b, g % NZ : g % NZ + 8, :] for n in range(4))
            over_n[b, g : g + 8, :] = a_n * rows[0, b, g : g + 8, :] + b_n * hn
            over_s[b, g : g + 8, :] = a_s * hs + b_s * rows[1, b, g : g + 8, :]
    leven = idx[1] == 1
    a, c = g1[...].astype(F32), g2[...].astype(F32)
    from_e, from_w = jnp.where(leven, a, c), jnp.where(leven, c, a)
    dl[0] = facec[0] * hnew[0] + facec[1] * from_e
    dl[1] = facec[2] * from_w + facec[3] * hnew[1]
    for b in range(NB):
        mix[b] = VMIX * wet[:, col(b)].astype(F32)
    lane = lanes()

    def ready(i):
        for r in range(NR):
            back = L - (r * NZ + i * CH)
            over_e, over_w = pltpu.roll(fluxes1[0], back, 1), pltpu.roll(fluxes1[1], back, 1)
            for h in range(CH):
                z = i * CH + h
                at = pl.ds(r * NZ + z, 1)
                for b in range(NB):
                    v = add_rows(first_in[b, r, z], fluxy[1, b, at, :], fluxy[0, b, at, :])
                    if b == 0:
                        v = v + jnp.where(lane == 0, pltpu.roll(over_w, (L - h) % L, 1), 0.0)
                    if b == NB - 1:
                        v = v - jnp.where(lane == L - 1, pltpu.roll(over_e, L - 1 - h, 1), 0.0)
                    first[b, r, z] = v

    ready(0)
    for b in range(NB):
        for r in range(NR):
            first[b, r, 0] = first[b, r, 0] + forcing[b, r]

    def level(h, z, over_e, over_w):
        coef = [[coefs[n, b, z] for b in range(NB)] for n in range(5)]

        def put(b, r, j, val):
            if b == 0:
                val = val + jnp.where(lane == 0, pltpu.roll(over_w[r], (L - h) % L, 1), 0.0)
            if b == NB - 1:
                val = val - jnp.where(lane == L - 1, pltpu.roll(over_e[r], L - 1 - h, 1), 0.0)
            at = pl.ds(j, 1)
            out_v[b, r, z] = add_rows(val, over_s[b, at, :], over_n[b, at, :])

        stencil(lambda b, r, zz: first[b, r, zz], coef, z, [mix[b] for b in range(NB)], put)

    def chunk(i, _):
        @pl.when(i < NC - 1)
        def _():
            ready(jnp.minimum(i + 1, NC - 1))

        over_e = [pltpu.roll(dl[0], L - (r * NZ + i * CH), 1) for r in range(NR)]
        over_w = [pltpu.roll(dl[1], L - (r * NZ + i * CH), 1) for r in range(NR)]
        for h in range(CH):
            level(h, i * CH + h, over_e, over_w)

        @pl.when(i == 0)
        def _():
            for b in range(NB):
                for r in range(NR):
                    out_v[b, r, 0] = out_v[b, r, 0] + forcing[b, r]

        for b in range(NB):
            copy(i, b).start()
        return 0

    lax.fori_loop(0, NC, chunk, 0)
    for i in range(NC):
        for b in range(NB):
            copy(i, b).wait()


def vmem(x):
    return pltpu.with_memory_space_constraint(x, pltpu.VMEM)


def hbm(x):
    return pltpu.with_memory_space_constraint(x, pltpu.HBM)


def shards(
    fluxes, tracers, diffusivity, east_speed, north_speed, wet, coupling, sources, live_slots, tiles
):
    sds = jax.ShapeDtypeStruct
    band, lon = lax.axis_index("comp"), lax.axis_index("lon")
    n_lon = lax.axis_size("lon")
    idx = jnp.stack([1 - band % 2, 1 - lon % 2, (lon + 1) % n_lon, (lon + n_lon - 1) % n_lon]).astype(jnp.int32)
    dma = pltpu.SemaphoreType.DMA
    q5, s5 = (NB, NR, NZ, NY, L), (NB, NZ, NY, L)
    cf = (5, NB, NZ, NY, L)
    nat, nats, tile = (NR, NZ, NY, 640), (NZ, NY, 640), (NB, NY, L)
    rowpay, edgepay = (NB, 208, L), (NB, 128, L)

    def params(mib):
        return pltpu.CompilerParams(vmem_limit_bytes=mib << 20)

    def cost(us):
        return pl.CostEstimate(flops=0, transcendentals=0, bytes_accessed=us * 3_000_000)

    flux, q, k, e, n, wh = map(
        hbm, (fluxes[:, 0, :], tracers, diffusivity, east_speed, north_speed, wet)
    )
    a2a, ns1, ns2, hown, edge_n, edge_s = pl.pallas_call(
        pack_kernel,
        out_shape=(
            sds((16, 8, NY, L), BF), sds(rowpay, BF), sds(rowpay, BF), sds((4, NY, L), F32),
            sds(rowpay, F32), sds(rowpay, F32),
        ),
        in_specs=[SM] + [ANY] * 6,
        out_specs=(VM,) * 6,
        scratch_shapes=[
            pltpu.VMEM((10, 12288), BF), pltpu.VMEM(q5, F32), pltpu.VMEM(s5, F32), pltpu.VMEM((NB, NZ, 8, L), F32),
            pltpu.VMEM((NZ, NY, L), F32), pltpu.VMEM((NY, 640), jnp.int32), dma((18,)),
        ],
        cost_estimate=cost(6),
        compiler_params=params(20),
        name="pack",
    )(idx, flux, q, k, e, n, wh)
    swap_a = [(i, i ^ 1) for i in range(8)]
    swap_b = [(i, i + 1) for i in (1, 3, 5)] + [(i + 1, i) for i in (1, 3, 5)]
    r1 = lax.ppermute(ns1, "comp", swap_a)
    r2 = lax.ppermute(ns2, "comp", swap_b)
    got = lax.all_to_all(a2a, "lon", split_axis=0, concat_axis=0, tiled=True)
    first, coefs, rows, cols = pl.pallas_call(
        step1_kernel,
        out_shape=(pltpu.HBM(q5, F32), pltpu.HBM(cf, F32), sds((2,) + edgepay, F32), sds((2, NY, L), F32)),
        in_specs=[ANY] * 5,
        out_specs=(ANY,) * 2 + (VM,) * 2,
        scratch_shapes=[
            pltpu.VMEM(nat, F32), pltpu.VMEM(nats, F32), pltpu.VMEM(nats, F32), pltpu.VMEM(nats, F32),
            pltpu.VMEM(q5, F32), pltpu.VMEM(cf, F32),
            pltpu.VMEM((NY, 640), jnp.int32),
            pltpu.VMEM(tile, F32), pltpu.VMEM(tile, F32), pltpu.VMEM(tile, F32), pltpu.VMEM(tile, F32),
            dma((N1 + 1, 4)), dma((N1, 2)),
        ],
        cost_estimate=cost(30),
        compiler_params=params(28),
        name="step1",
    )(wh, q, k, e, n)
    forcing, ms1, ms2, ew1, ew2, hnew, facec, fluxes1, rows, facey, fluxy = pl.pallas_call(
        remap_kernel,
        out_shape=(
            sds((NB, NR, NY, L), F32), sds(edgepay, BF), sds(edgepay, BF), sds((NY, L), BF), sds((NY, L), BF),
            sds((2, NY, L), F32), sds((4, NY, L), F32), sds((2, NY, L), F32),
            sds((2,) + edgepay, F32), sds((4, NB, NZ, L), F32), sds((2,) + edgepay, F32),
        ),
        in_specs=[SM] * 4 + [VM, ANY] + [VM] * 8,
        out_specs=(VM,) * 11,
        scratch_shapes=[pltpu.VMEM((80, 512, L), BF), dma((NY,))],
        cost_estimate=cost(7),
        compiler_params=params(20),
        name="remap",
    )(idx, sources.T, live_slots, coupling, got.reshape(128, NY, L), hbm(tiles.reshape(80, 512, L)), wet, hown, rows, cols,
      edge_n, edge_s, r1, r2)
    lon_a = [(i, i ^ 1) for i in range(16)]
    lon_b = [((2 * i + 1) % 16, (2 * i + 2) % 16) for i in range(8)]
    lon_b = lon_b + [(b, a) for a, b in lon_b]
    r1 = lax.ppermute(ms1, "comp", swap_a)
    r2 = lax.ppermute(ms2, "comp", swap_b)
    g1 = lax.ppermute(ew1, "lon", lon_a)
    g2 = lax.ppermute(ew2, "lon", lon_b)
    return pl.pallas_call(
        step2_kernel,
        out_shape=sds(tracers.shape, F32),
        in_specs=[SM] + [VM] * 14,
        out_specs=ANY,
        scratch_shapes=[
            pltpu.VMEM(edgepay, F32), pltpu.VMEM(edgepay, F32), pltpu.VMEM(q5, F32), pltpu.VMEM(q5, F32),
            pltpu.VMEM((2, NY, L), F32), pltpu.VMEM(tile, F32), dma((NC, NB)),
        ],
        cost_estimate=cost(7),
        compiler_params=params(14),
        name="step2",
    )(idx, r1, r2, g1, g2, wet, forcing, hnew, facec, fluxes1, rows, facey, fluxy, vmem(coefs), vmem(first))


def solution(mesh):
    return jax.shard_map(
        shards,
        mesh=mesh,
        in_specs=(
            P(None, ("comp", "lon"), None),
            P(None, None, "comp", "lon"),
            P(None, "comp", "lon"),
            P(None, "comp", "lon"),
            P(None, "comp", "lon"),
            P("comp", "lon"),
            P(),
            P(("comp", "lon"), None),
            P(("comp", "lon")),
            P(("comp", "lon"), None, None, None),
        ),
        out_specs=P(None, None, "comp", "lon"),
        check_vma=False,
    )
```
